256 devices in a mesh: blk: 128 (over y, z, x_hi, core), dp: 2 (over x_lo).
Axes of the slice: x: 4 (x_hi: 2, x_lo: 2; x = x_hi * 2 + x_lo), y: 4, z: 8, core: 2. Of those that a mesh axis runs over, the one named last changes fastest.
Arguments:
- tokens: bfloat16 [32768, 3584], P(('blk', 'dp')), may hold values from -6 to 6
- route_dir: int32 [32768, 1], P(('blk', 'dp')), may hold values from 0 to 2; in each aligned block of 128 rows (0 to 127, 128 to 255, ...) at most 64 rows name the same one
- gate_probs: float32 [32768, 1], P(('blk', 'dp')), may hold values from 0.3 to 1
- gate_weight: bfloat16 [128, 3584, 512], P('blk', 'dp'), may hold values from -0.09375 to 0.09375
- up_weight: bfloat16 [128, 3584, 512], P('blk', 'dp'), may hold values from -0.09375 to 0.09375
- down_weight: bfloat16 [128, 3584, 512], P('blk', 'dp'), may hold values from -0.1875 to 0.1875
Outputs:
- d_tokens: bfloat16 [32768, 3584], P(('blk', 'dp'))
- grad_gate: bfloat16 [128, 3584, 512], P('blk', 'dp')
- grad_up: bfloat16 [128, 3584, 512], P('blk', 'dp')
- grad_down: bfloat16 [128, 3584, 512], P('blk', 'dp')
The draws below stay inside these ranges and needn't reach their ends.
Inputs may be any that keep to these rules, and one draw needn't show every extreme that they name: A token on blk index b sends its row to expert e = (b // 2 + route_dir - 1) mod 64, whose halves sit at blk indices 2e and 2e + 1; on one device at most 64 tokens take the same value.
All inputs are finite; a program needn't handle non-finite values.
Results may differ from the reference program's by a relative error of at most 0.0079.
Values may be sent and summed in bfloat16 or wider, within the bound.
No kernel may reach another device: no remote copies, remote signals or barrier semaphores. Data moves between devices by JAX's collectives and lax.ppermute only.
A program may use at most 128 MiB of HBM per device.

```python
import math
import jax
import jax.numpy as jnp
import numpy as np
from jax import lax

D = 3584
FF = 1024
TOK_DEV = 128
HALF = 512
CAP = 64
EXPERTS = 64
TOKENS = 32768
N_BLK = 128
N_DP = 2


def block_levels(stream_key, dims, split, least, largest):
    factor_of = 1.0
    for position, parts in split:
        draws = jax.random.uniform(jax.random.fold_in(jax.random.fold_in(stream_key, 6), position), (parts,), jnp.float32, least / len(split), largest / len(split))
        factor_of = factor_of * jnp.repeat(jnp.exp(draws), dims[position] // parts).reshape((-1,) + (1,) * (len(dims) - 1 - position))
    return factor_of


def deal_out(key, own, number, rows, number_of, top, bound, skew):
    sequence = jax.random.permutation(key, number_of)
    crowded, ordinary = portions_of(number_of, rows * top, bound, skew, True), portions_of(number_of, rows * top, bound, skew, False)
    places = jnp.arange(number_of)

    def named(sizes, rotation):
        used = int((sizes > 0).sum())
        fixed = max(1, used // 4)
        moved = fixed + (places - fixed + rotation * (used - fixed)) % max(1, number_of - fixed)
        return jnp.zeros((number_of,), jnp.int32).at[sequence[jnp.where(places < fixed, places, moved)]].set(jnp.asarray(sizes, jnp.int32))

    sizes = jnp.where(number % 4 == 0, named(crowded, number // 4), named(ordinary, number - number // 4 - 1))
    mixed = jax.random.permutation(jax.random.fold_in(own, 3), number_of)
    donor, taker = mixed[0:number_of // 2 * 2:2], mixed[1:number_of // 2 * 2:2]
    margin = jnp.minimum(sizes[donor] - 1, bound - sizes[taker]) // 2
    margin = jnp.where((donor == sequence[0]) | (taker == sequence[0]) | (sizes[taker] == 0), 0, jnp.maximum(margin, 0))
    moved = jax.random.randint(jax.random.fold_in(own, 4), (number_of // 2,), 0, 1 << 20) % (margin + 1)
    sizes = sizes.at[donor].add(-moved).at[taker].add(moved)
    labels = jnp.searchsorted(jnp.cumsum(sizes), jnp.arange(rows * top), side="right").astype(jnp.int32)
    listing = labels.reshape(top, rows).T
    listing = listing[jax.random.permutation(jax.random.fold_in(own, 1), rows)]
    rotation = jax.random.randint(jax.random.fold_in(own, 2), (rows, 1), 0, top)
    return jnp.take_along_axis(listing, (jnp.arange(top)[None, :] + rotation) % top, axis=1)


def portions_of(number_of, total, bound, slope, full):
    portions = [(1 << 20) // math.isqrt(rank ** slope) + 1 for rank in range(1, number_of + 1)]
    largest = bound if full else min(bound, max(-(-total // number_of), total * portions[0] // sum(portions)))
    least = 1 if total - largest >= number_of - 1 else 0
    counts, surplus = [largest] + [least] * (number_of - 1), total - largest - least * (number_of - 1)
    while surplus > 0:
        free = [i for i in range(1, number_of) if counts[i] < largest] or [i for i in range(1, number_of) if counts[i] < bound]
        whole, remaining = sum([portions[i] for i in free]), surplus
        for i in free:
            more = min(bound - counts[i], max(1, remaining * portions[i] // whole), surplus)
            counts[i] = counts[i] + more
            surplus = surplus - more
    return np.array(counts)


def centred(stream_key, shape, deviation, bound, shards=(), kind=jnp.bfloat16):
    gain = block_levels(stream_key, shape, shards, -0.22, 0.18) if shards else 1.0
    values = jax.random.normal(stream_key, shape, jnp.float32) * deviation * gain
    return jnp.minimum(jnp.maximum(values, -bound), bound).astype(kind)


def setup_inputs(seed: int = 0) -> dict:
    keys = jax.random.split(jax.random.key(seed), 7)
    tokens = centred(keys[0], (TOKENS, D), 1.0, 6.0, ((0, 256),))
    route_dir_keys = jax.random.split(jax.random.fold_in(keys[1], 1), TOKENS // TOK_DEV)
    route_dir_turns = jax.random.permutation(jax.random.fold_in(keys[1], 3), TOKENS // TOK_DEV)
    route_dir = jax.vmap(lambda own, number: deal_out(jax.random.fold_in(keys[1], 2), own, number, TOK_DEV, 3, 1, CAP, 2))(route_dir_keys, route_dir_turns).reshape((TOKENS, 1))
    gate_probs = jnp.clip(0.3 + 0.7 * jax.random.uniform(keys[2], (TOKENS, 1), jnp.float32) ** block_levels(keys[2], (TOKENS, 1), ((0, 256),), -0.2, 0.2), 0.3, 1.0)
    gate_weight = centred(keys[3], (2 * EXPERTS, D, HALF), D ** -0.5, 0.09375, ((0, 128), (1, 2)))
    up_weight = centred(keys[4], (2 * EXPERTS, D, HALF), D ** -0.5, 0.09375, ((0, 128), (1, 2)))
    down_weight = centred(keys[5], (2 * EXPERTS, D, HALF), FF ** -0.5, 0.1875, ((0, 128), (1, 2)))
    return {"tokens": tokens, "route_dir": route_dir, "gate_probs": gate_probs, "gate_weight": gate_weight, "up_weight": up_weight, "down_weight": down_weight}


def selection(directions, capacity):
    slot_ids = jnp.arange(capacity, dtype=jnp.int32)
    planes = []
    for direction in range(3):
        chosen = (directions == direction).astype(jnp.int32)
        places = jnp.cumsum(chosen, axis=-1, dtype=jnp.int32) - 1
        matches = (chosen[..., None, :] == 1) & (places[..., None, :] == slot_ids[:, None])
        planes.append(matches)
    return jnp.stack(planes, axis=-3).astype(jnp.bfloat16)

def round_trip(payload):
    return lax.optimization_barrier(payload.astype(jnp.bfloat16)).astype(jnp.float32)

def matmul(left_side, right_side):
    return jnp.dot(left_side, right_side, preferred_element_type=jnp.float32)

def times_transposed(left_side, right_side):
    return lax.dot_general(left_side, right_side, (((1,), (1,)), ((), ())), preferred_element_type=jnp.float32)

def activate(pre_gate, pre_up):
    sigmoid = jax.nn.sigmoid(pre_gate)
    return ((pre_gate * sigmoid * pre_up).astype(jnp.bfloat16), sigmoid)

def hidden_grads(d_hidden, pre_gate, pre_up, sigmoid):
    d_gate = (d_hidden * pre_up * (sigmoid * (1.0 + pre_gate * (1.0 - sigmoid)))).astype(jnp.bfloat16)
    d_up = (d_hidden * (pre_gate * sigmoid)).astype(jnp.bfloat16)
    return (d_gate, d_up)

def group_grad(left_side, right_side, groups):
    lhs_float = left_side.reshape(groups, -1, left_side.shape[-1]).astype(jnp.float32)
    rhs_float = right_side.reshape(groups, -1, right_side.shape[-1]).astype(jnp.float32)
    group_terms = jnp.einsum('grk,grh->gkh', lhs_float, rhs_float)
    return lax.optimization_barrier(jnp.sum(round_trip(group_terms), axis=0)).astype(jnp.bfloat16)

def reference(tokens, route_dir, gate_probs, gate_weight, up_weight, down_weight):
    blocks = tokens.reshape(N_BLK, N_DP, TOK_DEV, D)
    directions = route_dir.reshape(N_BLK, N_DP, TOK_DEV)
    weights_in = gate_probs.reshape(N_BLK, N_DP, TOK_DEV)
    selector = selection(directions, CAP)
    offsets = jnp.array([2, 3, 0, 1, -2, -1], dtype=jnp.int32)
    side_ids = jnp.array([0, 0, 1, 1, 2, 2], dtype=jnp.int32)
    row_count = N_DP * 6 * CAP

    def one_expert(expert):
        sources = (offsets + 2 * expert) % N_BLK
        chosen = selector[sources, :, side_ids].astype(jnp.float32)
        gathered = jnp.einsum('ndst,ndtk->ndsk', chosen, blocks[sources].astype(jnp.float32)).astype(jnp.bfloat16)
        scales = jnp.einsum('ndst,ndt->nds', chosen, weights_in[sources])
        inputs = gathered.transpose(1, 0, 2, 3).reshape(row_count, D)
        scales = scales.transpose(1, 0, 2).reshape(row_count, 1)
        stored = []
        partial_sum = jnp.zeros((row_count, D), jnp.float32)
        for which_half in range(2):
            member = 2 * expert + which_half
            w_gate = lax.dynamic_index_in_dim(gate_weight, member, 0, keepdims=False)
            w_up = lax.dynamic_index_in_dim(up_weight, member, 0, keepdims=False)
            w_down = lax.dynamic_index_in_dim(down_weight, member, 0, keepdims=False)
            pre_gate = matmul(inputs, w_gate)
            pre_up = matmul(inputs, w_up)
            activated, sigmoid = activate(pre_gate, pre_up)
            partial_sum = partial_sum + round_trip(times_transposed(activated, w_down))
            stored.append((w_gate, w_up, w_down, pre_gate, pre_up, activated, sigmoid))
        result = scales * round_trip(partial_sum)
        back_rows = (scales * result).astype(jnp.bfloat16)
        grads_gate = []
        grads_up = []
        grads_down = []
        dx_sum = jnp.zeros((row_count, D), jnp.float32)
        for w_gate, w_up, w_down, pre_gate, pre_up, activated, sigmoid in stored:
            d_hidden = matmul(back_rows, w_down)
            d_gate, d_up = hidden_grads(d_hidden, pre_gate, pre_up, sigmoid)
            grads_gate.append(group_grad(inputs, d_gate, N_DP))
            grads_up.append(group_grad(inputs, d_up, N_DP))
            grads_down.append(group_grad(back_rows, activated, N_DP))
            dx_sum = dx_sum + round_trip(times_transposed(d_gate, w_gate) + times_transposed(d_up, w_up))
        dx_rows = dx_sum.astype(jnp.bfloat16).reshape(N_DP, 6, CAP, D).transpose(1, 0, 2, 3)
        return (dx_rows, jnp.stack(grads_gate), jnp.stack(grads_up), jnp.stack(grads_down))
    dx_rows, grads_gate, grads_up, grads_down = lax.map(one_expert, jnp.arange(EXPERTS, dtype=jnp.int32))

    def one_source(source):
        pieces = []
        for direction in range(3):
            expert = (source // 2 + direction - 1) % EXPERTS
            slot_id = 2 * direction + source % 2
            pieces.append(dx_rows[expert, slot_id])
        stacked = jnp.stack(pieces, axis=1)
        return jnp.einsum('djst,djsk->dtk', selector[source].astype(jnp.float32), stacked.astype(jnp.float32)).astype(jnp.bfloat16)
    d_tokens = lax.map(one_source, jnp.arange(N_BLK, dtype=jnp.int32)).reshape(TOKENS, D)
    shape_out = (2 * EXPERTS, D, HALF)
    return (d_tokens, grads_gate.reshape(shape_out), grads_up.reshape(shape_out), grads_down.reshape(shape_out))
```

```python
import functools

import jax
import jax.numpy as jnp
from jax import lax
from jax.experimental import pallas as pl
from jax.experimental.pallas import tpu as pltpu
from jax.sharding import PartitionSpec as P

CAP = 64
EXTRA = 128
BF16 = jnp.bfloat16
F32 = jnp.float32
PARAMS = pltpu.CompilerParams(vmem_limit_bytes=20 * 1024 * 1024)
SMALL = pltpu.CompilerParams(vmem_limit_bytes=12 * 1024 * 1024)


def dot(a, b):
    return lax.dot_general(a, b, (((1,), (0,)), ((), ())), preferred_element_type=F32)


def dot_t(a, b):
    return lax.dot_general(a, b, (((1,), (1,)), ((), ())), preferred_element_type=F32)


def t_dot(a, b):
    return lax.dot_general(a, b, (((0,), (0,)), ((), ())), preferred_element_type=F32)


def send(x, by, flip, tag):
    n, m = lax.axis_size("blk"), lax.axis_size("dp")
    route = [(b * m + d, ((b + by) % n) * m + (d ^ flip)) for b in range(n) for d in range(m)]
    with jax.named_scope(tag):
        return lax.ppermute(x, ("blk", "dp"), route)


def swap_dp(x, tag):
    with jax.named_scope(tag):
        return lax.ppermute(x, "dp", [(0, 1), (1, 0)])


def swap_core(x, tag):
    with jax.named_scope(tag):
        return lax.ppermute(x, "blk", [(i, i ^ 1) for i in range(lax.axis_size("blk"))])


def after(x, *earlier):
    return lax.optimization_barrier((x,) + earlier)[0]


def select_kernel(d_ref, tokens, route, gate, sel_ref, *outs):
    count, width = tokens.shape
    half = width // 2
    d = d_ref[0]
    row = lax.broadcasted_iota(jnp.int32, (count, count), 0)
    col = lax.broadcasted_iota(jnp.int32, (count, count), 1)
    upper = jnp.where(row <= col, 1.0, 0.0).astype(BF16)
    chosen = jnp.where(route[...] == row, 1.0, 0.0)
    counts = dot(chosen.astype(BF16), upper)
    slot = lax.broadcasted_iota(jnp.int32, (CAP, count), 0).astype(F32)
    lane = lax.broadcasted_iota(jnp.int32, (CAP, EXTRA), 1)
    for j in range(3):
        hit = (chosen[j : j + 1, :] > 0.5) & (counts[j : j + 1, :] - 1.0 == slot)
        value = jnp.sum(jnp.where(hit, gate[...], 0.0), axis=1, keepdims=True)
        high = value.astype(BF16).astype(F32)
        picked = jnp.where(lane == 0, high, jnp.where(lane == 1, value - high, 0.0)).astype(BF16)
        sel = jnp.where(hit, 1.0, 0.0).astype(BF16)
        sel_ref[j * CAP : (j + 1) * CAP, :] = sel
        for k, which in enumerate((d, 1 - d)):
            at = pl.multiple_of(which * half, 128)
            outs[2 * j + k][:, :half] = dot(sel, tokens[:, pl.ds(at, half)]).astype(BF16)
            outs[2 * j + k][:, half:] = picked


def select(d, tokens, route_dir, gate_probs):
    count, width = tokens.shape
    piece = jax.ShapeDtypeStruct((CAP, width // 2 + EXTRA), BF16)
    vmem = pl.BlockSpec(memory_space=pltpu.VMEM)
    return pl.pallas_call(
        select_kernel,
        out_shape=(jax.ShapeDtypeStruct((3 * CAP, count), BF16),) + (piece,) * 6,
        in_specs=[pl.BlockSpec(memory_space=pltpu.SMEM), vmem, vmem, vmem],
        out_specs=(vmem,) * 7,
        compiler_params=PARAMS,
        name="select",
    )(d, tokens, route_dir.reshape(1, count), gate_probs.reshape(1, count))


def reorder(x):
    return jnp.concatenate([x[CAP * i : CAP * (i + 1)] for i in (1, 0, 3, 2)], axis=0)


def both(sent, got):
    return reorder(sent[...]).astype(F32) + got[...].astype(F32)


def pre_kernel(a, b, c, d, wg, wu, x_out, gates, out):
    width, f = wg.shape
    pieces = (a, b, c, d)
    x = jnp.concatenate([p[:, :width] for p in pieces], axis=0)
    x_out[...] = x
    gates[...] = jnp.concatenate([p[:, width:] for p in pieces], axis=0)
    for k, w in enumerate((wg, wu)):
        out[:, k * f : (k + 1) * f] = reorder(dot(x, w[...]).astype(BF16))


def pre(pieces, wg, wu):
    rows, (width, f) = 4 * CAP, wg.shape
    return pl.pallas_call(
        pre_kernel,
        out_shape=(
            jax.ShapeDtypeStruct((rows, width), BF16),
            jax.ShapeDtypeStruct((rows, EXTRA), BF16),
            jax.ShapeDtypeStruct((rows, 2 * f), BF16),
        ),
        compiler_params=SMALL,
        name="pre",
    )(*pieces, wg, wu)


def down_kernel(sent, got, wd, hidden, part):
    f = wd.shape[1]
    value = both(sent, got)
    pg, pu = value[:, :f], value[:, f:]
    h = (pg * jax.nn.sigmoid(pg) * pu).astype(BF16)
    hidden[...] = h
    value = dot_t(h, wd[...]).astype(BF16)
    rows = value.shape[0] // 2
    part[:rows] = value[rows:]
    part[rows:] = value[:rows]


def down(sent, got, wd):
    rows = sent.shape[0]
    width, f = wd.shape
    return pl.pallas_call(
        down_kernel,
        out_shape=(
            jax.ShapeDtypeStruct((rows, f), BF16),
            jax.ShapeDtypeStruct((rows, width), BF16),
        ),
        compiler_params=SMALL,
        name="down",
    )(sent, got, wd)


def turn_kernel(part, got, gates, wd, back_out, dh):
    rows = part.shape[0] // 2
    own = jnp.concatenate([part[rows:], part[:rows]], axis=0)
    expert_out = own.astype(F32) + got[...].astype(F32)
    gate = gates[:, 0:1].astype(F32) + gates[:, 1:2].astype(F32)
    back = (gate * (gate * expert_out)).astype(BF16)
    back_out[...] = back
    dh[...] = reorder(dot(back, wd[...]).astype(BF16))


def turn(part, got, gates, wd):
    rows = part.shape[0]
    width, f = wd.shape
    return pl.pallas_call(
        turn_kernel,
        out_shape=(
            jax.ShapeDtypeStruct((rows, width), BF16),
            jax.ShapeDtypeStruct((rows, f), BF16),
        ),
        compiler_params=SMALL,
        name="turn",
    )(part, got, gates, wd)


def back_kernel(sent, got, dh_sent, dh_got, wg, wu, acts, own, part):
    f = wg.shape[1]
    value = both(sent, got)
    pg, pu = value[:, :f], value[:, f:]
    dh = both(dh_sent, dh_got)
    s = jax.nn.sigmoid(pg)
    dg = (dh * pu * (s * (1.0 + pg * (1.0 - s)))).astype(BF16)
    du = (dh * (pg * s)).astype(BF16)
    acts[:, :f] = dg
    acts[:, f:] = du
    value = (dot_t(dg, wg[...]) + dot_t(du, wu[...])).astype(BF16)
    rows = value.shape[0] // 2
    own[...] = value[:rows]
    part[...] = value[rows:]


def back(sent, got, dh_sent, dh_got, wg, wu):
    rows = sent.shape[0]
    width, f = wg.shape
    half = jax.ShapeDtypeStruct((rows // 2, width), BF16)
    return pl.pallas_call(
        back_kernel,
        out_shape=(jax.ShapeDtypeStruct((rows, 2 * f), BF16), half, half),
        compiler_params=SMALL,
        name="back",
    )(sent, got, dh_sent, dh_got, wg, wu)


def add_kernel(own, got, same, other):
    value = (own[...].astype(F32) + got[...].astype(F32)).astype(BF16)
    same[...] = value[:CAP]
    other[...] = value[CAP:]


def add(own, got):
    piece = jax.ShapeDtypeStruct((CAP, own.shape[1]), BF16)
    return pl.pallas_call(
        add_kernel, out_shape=(piece, piece), compiler_params=SMALL, name="add"
    )(own, got)


def unpack_kernel(d_ref, sel, s0, s1, s2, o0, o1, o2, out):
    half = s0.shape[1]
    d = d_ref[0]
    for which, parts in ((d, (s0, s1, s2)), (1 - d, (o0, o1, o2))):
        at = pl.multiple_of(which * half, 128)
        rows = jnp.concatenate([p[...] for p in parts], axis=0)
        out[:, pl.ds(at, half)] = t_dot(sel[...], rows).astype(BF16)


def unpack(d, sel, same, other):
    count, half = sel.shape[1], same[0].shape[1]
    vmem = pl.BlockSpec(memory_space=pltpu.VMEM)
    return pl.pallas_call(
        unpack_kernel,
        out_shape=jax.ShapeDtypeStruct((count, 2 * half), BF16),
        in_specs=[pl.BlockSpec(memory_space=pltpu.SMEM)] + [vmem] * 7,
        out_specs=vmem,
        compiler_params=PARAMS,
        name="unpack",
    )(d, sel, *same, *other)


def grads_kernel(counts, *refs):
    groups = []
    for n in counts:
        groups.append(jnp.concatenate([r[...] for r in refs[:n]], axis=0))
        refs = refs[n:]
    x, acts, back_rows, hidden = groups
    gate_out, up_out, down_out = refs
    f = hidden.shape[1]
    up = t_dot(x, acts).astype(BF16)
    gate_out[...] = up[:, :f]
    up_out[...] = up[:, f:]
    down_out[...] = t_dot(back_rows, hidden).astype(BF16)


def grads(xs, acts, backs, hidden):
    width, f, tile = backs[0].shape[1], hidden[0].shape[1], 256

    def whole(x):
        return pl.BlockSpec(x.shape, lambda i: (0, 0))

    def columns(x):
        return pl.BlockSpec((x.shape[0], tile), lambda i: (0, i))

    out = pl.BlockSpec((tile, f), lambda i: (i, 0))
    return pl.pallas_call(
        functools.partial(grads_kernel, (len(xs), len(acts), len(backs), len(hidden))),
        grid=(width // tile,),
        in_specs=[columns(x) for x in xs]
        + [whole(x) for x in acts]
        + [columns(x) for x in backs]
        + [whole(x) for x in hidden],
        out_specs=[out] * 3,
        out_shape=[jax.ShapeDtypeStruct((width, f), BF16)] * 3,
        compiler_params=PARAMS,
        name="grads",
    )(*xs, *acts, *backs, *hidden)


def per_device(tokens, route_dir, gate_probs, gate_weight, up_weight, down_weight):
    d = lax.axis_index("dp").astype(jnp.int32).reshape(1)
    yes = d[0] < 2
    wg, wu, wd = gate_weight[0], up_weight[0], down_weight[0]

    def together(f, *args):
        shapes = jax.eval_shape(f, *args)

        def zeros(*_):
            return jax.tree.map(lambda s: jnp.zeros(s.shape, s.dtype), shapes)

        return lax.cond(yes, f, zeros, *args)

    def first(xs, xo, wg, wu):
        return pre((xs, xo, swap_core(xs, "cs"), swap_core(xo, "cx")), wg, wu)

    def middle(sent, got, gates, wd):
        h, part = down(sent, got, wd)
        return h, *turn(part, swap_core(part, "eo"), gates, wd)

    def last(sent, got, dh, dg, wg, wu):
        acts, own, part = back(sent, got, dh, dg, wg, wu)
        return acts, *add(own, swap_core(part, "dx"))

    sel, p_s, p_o, o_s, o_o, n_s, n_o = select(d, tokens, route_dir, gate_probs)
    o_x = swap_dp(o_o, "xO")
    p_x, p_y = send(p_o, -2, 1, "xPx"), send(p_s, -2, 0, "xPy")
    n_x, n_y = send(n_o, 2, 1, "xNx"), send(n_s, 2, 0, "xNy")
    x_o, g_o, e_o = together(first, o_s, o_x, wg, wu)
    got_o = swap_dp(e_o, "preO")
    x_p, g_p, e_p = together(first, after(p_y, g_o), p_x, wg, wu)
    got_p = swap_dp(e_p, "preP")
    x_n, g_n, e_n = together(first, after(n_y, g_p), n_x, wg, wu)
    got_n = swap_dp(e_n, "preN")
    h_o, r_o, u_o = together(middle, e_o, after(got_o, g_n), g_o, wd)
    dg_o = swap_dp(u_o, "dhO")
    h_p, r_p, u_p = together(middle, e_p, after(got_p, u_o), g_p, wd)
    dg_p = swap_dp(u_p, "dhP")
    h_n, r_n, u_n = together(middle, e_n, after(got_n, u_p), g_n, wd)
    dg_n = swap_dp(u_n, "dhN")
    a_o, os, oo = together(last, e_o, got_o, u_o, after(dg_o, u_n), wg, wu)
    o_o = swap_dp(oo, "rO")
    a_p, ps, po = together(last, e_p, got_p, u_p, after(dg_p, a_o), wg, wu)
    p_s, p_o = send(ps, 2, 0, "rPs"), send(po, 2, 1, "rPo")
    a_n, ns, no = together(last, e_n, got_n, u_n, after(dg_n, a_p), wg, wu)
    n_s, n_o = send(ns, -2, 0, "rNs"), send(no, -2, 1, "rNo")
    gg, gu, gd = grads((x_o, x_p, x_n), (a_o, a_p, a_n), (r_o, r_p, r_n), (h_o, h_p, h_n))
    d_tokens = unpack(d, after(sel, gd), (p_s, os, n_s), (p_o, o_o, n_o))
    return (d_tokens, gg[None], gu[None], gd[None])


def solution(mesh):
    return jax.shard_map(
        per_device,
        mesh=mesh,
        in_specs=(
            P(("blk", "dp"), None),
            P(("blk", "dp"), None),
            P(("blk", "dp"), None),
            P("blk", "dp", None),
            P("blk", "dp", None),
            P("blk", "dp", None),
        ),
        out_specs=(
            P(("blk", "dp"), None),
            P("blk", "dp", None),
            P("blk", "dp", None),
            P("blk", "dp", None),
        ),
        check_vma=False,
    )
```

```python
import functools

import jax
import jax.numpy as jnp
from jax import lax
from jax.experimental import pallas as pl
from jax.experimental.pallas import tpu as pltpu
from jax.sharding import PartitionSpec as P

CAP = 64
EXTRA = 128
BF16 = jnp.bfloat16
F32 = jnp.float32
PARAMS = pltpu.CompilerParams(vmem_limit_bytes=20 * 1024 * 1024)
SMALL = pltpu.CompilerParams(vmem_limit_bytes=10 * 1024 * 1024)


def dot(a, b):
    return lax.dot_general(a, b, (((1,), (0,)), ((), ())), preferred_element_type=F32)


def dot_t(a, b):
    return lax.dot_general(a, b, (((1,), (1,)), ((), ())), preferred_element_type=F32)


def t_dot(a, b):
    return lax.dot_general(a, b, (((0,), (0,)), ((), ())), preferred_element_type=F32)


def send(x, by, flip, tag):
    n, m = lax.axis_size("blk"), lax.axis_size("dp")
    route = [(b * m + d, ((b + by) % n) * m + (d ^ flip)) for b in range(n) for d in range(m)]
    with jax.named_scope(tag):
        return lax.ppermute(x, ("blk", "dp"), route)


def swap_dp(x, tag):
    with jax.named_scope(tag):
        return lax.ppermute(x, "dp", [(0, 1), (1, 0)])


def swap_core(x, tag):
    with jax.named_scope(tag):
        return lax.ppermute(x, "blk", [(i, i ^ 1) for i in range(lax.axis_size("blk"))])


def after(x, *earlier):
    return lax.optimization_barrier((x,) + earlier)[0]


def select_kernel(d_ref, tokens, route, gate, sel_ref, *outs):
    count, width = tokens.shape
    half = width // 2
    d = d_ref[0]
    row = lax.broadcasted_iota(jnp.int32, (count, count), 0)
    col = lax.broadcasted_iota(jnp.int32, (count, count), 1)
    upper = jnp.where(row <= col, 1.0, 0.0).astype(BF16)
    chosen = jnp.where(route[...] == row, 1.0, 0.0)
    counts = dot(chosen.astype(BF16), upper)
    slot = lax.broadcasted_iota(jnp.int32, (CAP, count), 0).astype(F32)
    lane = lax.broadcasted_iota(jnp.int32, (CAP, EXTRA), 1)
    for j in range(3):
        hit = (chosen[j : j + 1, :] > 0.5) & (counts[j : j + 1, :] - 1.0 == slot)
        value = jnp.sum(jnp.where(hit, gate[...], 0.0), axis=1, keepdims=True)
        high = value.astype(BF16).astype(F32)
        picked = jnp.where(lane == 0, high, jnp.where(lane == 1, value - high, 0.0)).astype(BF16)
        sel = jnp.where(hit, 1.0, 0.0).astype(BF16)
        sel_ref[j * CAP : (j + 1) * CAP, :] = sel
        for k, which in enumerate((d, 1 - d)):
            at = pl.multiple_of(which * half, 128)
            outs[2 * j + k][:, :half] = dot(sel, tokens[:, pl.ds(at, half)]).astype(BF16)
            outs[2 * j + k][:, half:] = picked


def select(d, tokens, route_dir, gate_probs):
    count, width = tokens.shape
    piece = jax.ShapeDtypeStruct((CAP, width // 2 + EXTRA), BF16)
    vmem = pl.BlockSpec(memory_space=pltpu.VMEM)
    return pl.pallas_call(
        select_kernel,
        out_shape=(jax.ShapeDtypeStruct((3 * CAP, count), BF16),) + (piece,) * 6,
        in_specs=[pl.BlockSpec(memory_space=pltpu.SMEM), vmem, vmem, vmem],
        out_specs=(vmem,) * 7,
        compiler_params=PARAMS,
        name="select",
    )(d, tokens, route_dir.reshape(1, count), gate_probs.reshape(1, count))


def reorder(x):
    return jnp.concatenate([x[CAP * i : CAP * (i + 1)] for i in (1, 0, 3, 2)], axis=0)


def both(sent, got):
    return reorder(sent[...]).astype(F32) + got[...].astype(F32)


STREAMS = 4


def fetch(pairs, sems):
    copies = []
    for i, (src, dst) in enumerate(pairs):
        n = src.shape[0] // STREAMS
        group = [
            pltpu.make_async_copy(
                src.at[pl.ds(j * n, n)], dst.at[pl.ds(j * n, n)], sems.at[i * STREAMS + j]
            )
            for j in range(STREAMS)
        ]
        for copy in group:
            copy.start()
        copies.append(group)
    return copies


def arrived(group):
    for copy in group:
        copy.wait()


def weight_specs(inputs, weights):
    return [pl.BlockSpec(memory_space=pltpu.VMEM)] * inputs + [
        pl.BlockSpec(memory_space=pltpu.HBM)
    ] * weights


def weight_scratch(w, n):
    return [pltpu.VMEM(w.shape, BF16)] * n + [pltpu.SemaphoreType.DMA((n * STREAMS,))]


def pre_kernel(a, b, c, d, wg_in, wu_in, x_out, gates, out, wg, wu, sems):
    copies = fetch(((wg_in, wg), (wu_in, wu)), sems)
    width, f = wg.shape
    pieces = (a, b, c, d)
    x = jnp.concatenate([p[:, :width] for p in pieces], axis=0)
    x_out[...] = x
    gates[...] = jnp.concatenate([p[:, width:] for p in pieces], axis=0)
    for k, w in enumerate((wg, wu)):
        arrived(copies[k])
        out[:, k * f : (k + 1) * f] = reorder(dot(x, w[...]).astype(BF16))


def pre(pieces, wg, wu):
    rows, (width, f) = 4 * CAP, wg.shape
    return pl.pallas_call(
        pre_kernel,
        out_shape=(
            jax.ShapeDtypeStruct((rows, width), BF16),
            jax.ShapeDtypeStruct((rows, EXTRA), BF16),
            jax.ShapeDtypeStruct((rows, 2 * f), BF16),
        ),
        in_specs=weight_specs(4, 2),
        scratch_shapes=weight_scratch(wg, 2),
        compiler_params=SMALL,
        name="pre",
    )(*pieces, wg, wu)


def down_kernel(sent, got, wd, hidden, part):
    f = wd.shape[1]
    value = both(sent, got)
    pg, pu = value[:, :f], value[:, f:]
    h = (pg * jax.nn.sigmoid(pg) * pu).astype(BF16)
    hidden[...] = h
    value = dot_t(h, wd[...]).astype(BF16)
    rows = value.shape[0] // 2
    part[:rows] = value[rows:]
    part[rows:] = value[:rows]


def down(sent, got, wd):
    rows = sent.shape[0]
    width, f = wd.shape
    return pl.pallas_call(
        down_kernel,
        out_shape=(
            jax.ShapeDtypeStruct((rows, f), BF16),
            jax.ShapeDtypeStruct((rows, width), BF16),
        ),
        compiler_params=SMALL,
        name="down",
    )(sent, got, wd)


def turn_kernel(part, got, gates, wd, back_out, dh):
    rows = part.shape[0] // 2
    own = jnp.concatenate([part[rows:], part[:rows]], axis=0)
    expert_out = own.astype(F32) + got[...].astype(F32)
    gate = gates[:, 0:1].astype(F32) + gates[:, 1:2].astype(F32)
    back = (gate * (gate * expert_out)).astype(BF16)
    back_out[...] = back
    dh[...] = reorder(dot(back, wd[...]).astype(BF16))


def turn(part, got, gates, wd):
    rows = part.shape[0]
    width, f = wd.shape
    return pl.pallas_call(
        turn_kernel,
        out_shape=(
            jax.ShapeDtypeStruct((rows, width), BF16),
            jax.ShapeDtypeStruct((rows, f), BF16),
        ),
        compiler_params=SMALL,
        name="turn",
    )(part, got, gates, wd)


def back_kernel(sent, got, dh_sent, dh_got, wg, wu, acts, own, part):
    f = wg.shape[1]
    value = both(sent, got)
    pg, pu = value[:, :f], value[:, f:]
    dh = both(dh_sent, dh_got)
    s = jax.nn.sigmoid(pg)
    dg = (dh * pu * (s * (1.0 + pg * (1.0 - s)))).astype(BF16)
    du = (dh * (pg * s)).astype(BF16)
    acts[:, :f] = dg
    acts[:, f:] = du
    value = (dot_t(dg, wg[...]) + dot_t(du, wu[...])).astype(BF16)
    rows = value.shape[0] // 2
    own[...] = value[:rows]
    part[...] = value[rows:]


def back(sent, got, dh_sent, dh_got, wg, wu):
    rows = sent.shape[0]
    width, f = wg.shape
    half = jax.ShapeDtypeStruct((rows // 2, width), BF16)
    return pl.pallas_call(
        back_kernel,
        out_shape=(jax.ShapeDtypeStruct((rows, 2 * f), BF16), half, half),
        compiler_params=SMALL,
        name="back",
    )(sent, got, dh_sent, dh_got, wg, wu)


def add_kernel(own, got, same, other):
    value = (own[...].astype(F32) + got[...].astype(F32)).astype(BF16)
    same[...] = value[:CAP]
    other[...] = value[CAP:]


def add(own, got):
    piece = jax.ShapeDtypeStruct((CAP, own.shape[1]), BF16)
    return pl.pallas_call(
        add_kernel, out_shape=(piece, piece), compiler_params=SMALL, name="add"
    )(own, got)


def unpack_kernel(d_ref, sel, s0, s1, s2, o0, o1, o2, out):
    half = s0.shape[1]
    d = d_ref[0]
    for which, parts in ((d, (s0, s1, s2)), (1 - d, (o0, o1, o2))):
        at = pl.multiple_of(which * half, 128)
        rows = jnp.concatenate([p[...] for p in parts], axis=0)
        out[:, pl.ds(at, half)] = t_dot(sel[...], rows).astype(BF16)


def unpack(d, sel, same, other):
    count, half = sel.shape[1], same[0].shape[1]
    vmem = pl.BlockSpec(memory_space=pltpu.VMEM)
    return pl.pallas_call(
        unpack_kernel,
        out_shape=jax.ShapeDtypeStruct((count, 2 * half), BF16),
        in_specs=[pl.BlockSpec(memory_space=pltpu.SMEM)] + [vmem] * 7,
        out_specs=vmem,
        compiler_params=PARAMS,
        name="unpack",
    )(d, sel, *same, *other)


def grads_kernel(counts, *refs):
    groups = []
    for n in counts:
        groups.append(jnp.concatenate([r[...] for r in refs[:n]], axis=0))
        refs = refs[n:]
    x, acts, back_rows, hidden = groups
    gate_out, up_out, down_out = refs
    f = hidden.shape[1]
    up = t_dot(x, acts).astype(BF16)
    gate_out[...] = up[:, :f]
    up_out[...] = up[:, f:]
    down_out[...] = t_dot(back_rows, hidden).astype(BF16)


def grads(xs, acts, backs, hidden):
    width, f, tile = backs[0].shape[1], hidden[0].shape[1], 256

    def whole(x):
        return pl.BlockSpec(x.shape, lambda i: (0, 0))

    def columns(x):
        return pl.BlockSpec((x.shape[0], tile), lambda i: (0, i))

    out = pl.BlockSpec((tile, f), lambda i: (i, 0))
    return pl.pallas_call(
        functools.partial(grads_kernel, (len(xs), len(acts), len(backs), len(hidden))),
        grid=(width // tile,),
        in_specs=[columns(x) for x in xs]
        + [whole(x) for x in acts]
        + [columns(x) for x in backs]
        + [whole(x) for x in hidden],
        out_specs=[out] * 3,
        out_shape=[jax.ShapeDtypeStruct((width, f), BF16)] * 3,
        compiler_params=PARAMS,
        name="grads",
    )(*xs, *acts, *backs, *hidden)


def per_device(tokens, route_dir, gate_probs, gate_weight, up_weight, down_weight):
    d = lax.axis_index("dp").astype(jnp.int32).reshape(1)
    yes = d[0] < 2
    wg, wu, wd = gate_weight[0], up_weight[0], down_weight[0]

    def together(f, *args):
        shapes = jax.eval_shape(f, *args)

        def zeros(*_):
            return jax.tree.map(lambda s: jnp.zeros(s.shape, s.dtype), shapes)

        return lax.cond(yes, f, zeros, *args)

    def first(xs, xo, wg, wu):
        return pre((xs, xo, swap_core(xs, "cs"), swap_core(xo, "cx")), wg, wu)

    def middle(sent, got, gates, wd):
        h, part = down(sent, got, wd)
        return h, *turn(part, swap_core(part, "eo"), gates, wd)

    def last(sent, got, dh, dg, wg, wu):
        acts, own, part = back(sent, got, dh, dg, wg, wu)
        return acts, *add(own, swap_core(part, "dx"))

    sel, p_s, p_o, o_s, o_o, n_s, n_o = select(d, tokens, route_dir, gate_probs)
    o_x = swap_dp(o_o, "xO")
    p_x, p_y = send(p_o, -2, 1, "xPx"), send(p_s, -2, 0, "xPy")
    n_x, n_y = send(n_o, 2, 1, "xNx"), send(n_s, 2, 0, "xNy")
    x_o, g_o, e_o = together(first, o_s, o_x, wg, wu)
    got_o = swap_dp(e_o, "preO")
    x_p, g_p, e_p = together(first, after(p_y, g_o), p_x, wg, wu)
    got_p = swap_dp(e_p, "preP")
    x_n, g_n, e_n = together(first, after(n_y, g_p), n_x, wg, wu)
    got_n = swap_dp(e_n, "preN")
    h_o, r_o, u_o = together(middle, e_o, after(got_o, g_n), g_o, wd)
    dg_o = swap_dp(u_o, "dhO")
    h_p, r_p, u_p = together(middle, e_p, after(got_p, u_o), g_p, wd)
    dg_p = swap_dp(u_p, "dhP")
    h_n, r_n, u_n = together(middle, e_n, after(got_n, u_p), g_n, wd)
    dg_n = swap_dp(u_n, "dhN")
    a_o, os, oo = together(last, e_o, got_o, u_o, after(dg_o, u_n), wg, wu)
    o_o = swap_dp(oo, "rO")
    a_p, ps, po = together(last, e_p, got_p, u_p, after(dg_p, a_o), wg, wu)
    p_s, p_o = send(ps, 2, 0, "rPs"), send(po, 2, 1, "rPo")
    a_n, ns, no = together(last, e_n, got_n, u_n, after(dg_n, a_p), wg, wu)
    n_s, n_o = send(ns, -2, 0, "rNs"), send(no, -2, 1, "rNo")
    gg, gu, gd = grads((x_o, x_p, x_n), (a_o, a_p, a_n), (r_o, r_p, r_n), (h_o, h_p, h_n))
    d_tokens = unpack(d, after(sel, gd), (p_s, os, n_s), (p_o, o_o, n_o))
    return (d_tokens, gg[None], gu[None], gd[None])


def solution(mesh):
    return jax.shard_map(
        per_device,
        mesh=mesh,
        in_specs=(
            P(("blk", "dp"), None),
            P(("blk", "dp"), None),
            P(("blk", "dp"), None),
            P("blk", "dp", None),
            P("blk", "dp", None),
            P("blk", "dp", None),
        ),
        out_specs=(
            P(("blk", "dp"), None),
            P("blk", "dp", None),
            P("blk", "dp", None),
            P("blk", "dp", None),
        ),
        check_vma=False,
    )
```
